256 devices in a mesh: lag: 32 (over x_hi, z, core), pts: 8 (over x_lo, y).
Axes of the slice: x: 4 (x_hi: 2, x_lo: 2; x = x_hi * 2 + x_lo), y: 4, z: 8, core: 2. Of those that a mesh axis runs over, the one named last changes fastest.
Arguments:
- history: bfloat16 [192, 2048, 128], P('lag'), may hold values from -6 to 6
- incident: bfloat16 [4, 2048, 128], P(None, 'pts'), may hold values from -6 to 6
- kernel_blocks: bfloat16 [49152, 128, 128], P(('lag', 'pts')), may hold values from -0.009765625 to 0.009765625
- block_row: int32 [49152], P(('lag', 'pts')), may hold values from 0 to 1
- block_col: int32 [49152], P(('lag', 'pts')), may hold values from 0 to 15
- lag_offset: int32 [49152], P(('lag', 'pts')), may hold values from 0 to 5
- mode_kernel: float32 [192, 128], P('lag'), may hold values from 0.25 to 2
- self_inverse: float32 [2048, 128], P('pts'), as said below
Outputs:
- densities: float32 [4, 2048, 128], P(None, 'pts')
The draws below stay inside these ranges and needn't reach their ends.
Inputs may be any that keep to these rules, and one draw needn't show every extreme that they name: Each point block of self_inverse is the identity plus independent entries.
All inputs are finite; a program needn't handle non-finite values.
Results may differ from the reference program's by a relative error of at most 0.00031.
Values may be sent and summed in bfloat16 or wider, within the bound.
No kernel may reach another device: no remote copies, remote signals or barrier semaphores. Data moves between devices by JAX's collectives and lax.ppermute only.
A program may use at most 128 MiB of HBM per device.

```python
import math
import jax
import jax.numpy as jnp
from jax import lax

MC = 128
B = 128
LAG_DEV = 6
NBLK = 192
STEPS = 4
PT_GROUPS = 8
NP = 2048
LAGS = 192
ROWB = 2
NCB = 16
BLOCKS = 49152


def pinned_draw(key, salt, upper):
    position = jnp.arange(BLOCKS, dtype=jnp.int32) % NBLK
    values = jax.random.randint(jax.random.fold_in(key, salt), (BLOCKS,), 0, upper, dtype=jnp.int32)
    values = jnp.where(position == 0, 0, jnp.where(position == 1, upper - 1, values))
    return values.astype(jnp.int32)


def draw_block_row(key, part):
    return pinned_draw(key, 11, ROWB)


def draw_block_col(key, part):
    return pinned_draw(key, 23, NCB)


def draw_lag_offset(key, part):
    return pinned_draw(key, 37, LAG_DEV)


def draw_self_inverse(key, part):
    identity = (jnp.arange(NP)[:, None] % B == jnp.arange(B)[None, :]).astype(jnp.float32)
    noise = 0.35 * jax.random.normal(jax.random.fold_in(key, 5), (NP, B), jnp.float32)
    return (identity + noise / jnp.sqrt(jnp.float32(B))).astype(jnp.float32)


def shard_levels(key, shape, pieces, low, top_value):
    level, own = 1.0, jax.random.fold_in(key, 6)
    for dim, blocks in pieces:
        heights = jnp.exp(jax.random.uniform(jax.random.fold_in(own, dim), (blocks,), jnp.float32, low / len(pieces), top_value / len(pieces)))
        level = level * jnp.repeat(heights, shape[dim] // blocks).reshape([-1 if axis == dim else 1 for axis in range(len(shape))])
    return level


def bell_draw(stream_key, dims, width, most, cuts=(), kind=jnp.bfloat16):
    values = jax.random.normal(stream_key, dims, jnp.float32) * width
    if len(cuts) > 0:
        values = shard_levels(stream_key, dims, cuts, -0.22, 0.18) * values
    return jnp.clip(values, min=-most, max=most).astype(kind)


def setup_inputs(seed: int = 0) -> dict:
    key_of = jax.random.split(jax.random.key(seed), 9)
    history = bell_draw(key_of[0], (LAGS, NP, MC), 1.0, 6.0, ((0, 32),))
    incident = bell_draw(key_of[1], (STEPS, NP, MC), 1.0, 6.0, ((1, 8),))
    kernel_blocks = bell_draw(key_of[2], (BLOCKS, B, B), (B * NBLK * LAGS // (ROWB * LAG_DEV)) ** -0.5, 0.009765625, ((0, 256),))
    block_row = draw_block_row(jax.random.fold_in(key_of[8], 71), 0)
    block_col = draw_block_col(jax.random.fold_in(key_of[8], 71), 0)
    lag_offset = draw_lag_offset(jax.random.fold_in(key_of[8], 71), 0)
    mode_kernel = jnp.clip(jnp.exp(math.log(2.0) - 2.0794415 * jax.random.uniform(key_of[6], (LAGS, MC), jnp.float32) ** shard_levels(key_of[6], (LAGS, MC), ((0, 32),), -0.2, 0.2)), 0.25, 2.0)
    self_inverse = draw_self_inverse(jax.random.fold_in(key_of[8], 71), 0)
    return dict(history=history, incident=incident, kernel_blocks=kernel_blocks, block_row=block_row, block_col=block_col, lag_offset=lag_offset, mode_kernel=mode_kernel, self_inverse=self_inverse)


def reference(history, incident, kernel_blocks, block_row, block_col, lag_offset, mode_kernel, self_inverse):
    owner_group = jnp.arange(BLOCKS, dtype=jnp.int32) // NBLK
    global_row = ((owner_group % PT_GROUPS) * ROWB + block_row).astype(jnp.int32)
    global_lag = ((owner_group // PT_GROUPS) * LAG_DEV + lag_offset).astype(jnp.int32)
    inverse_blocks = self_inverse.reshape(NCB, B, B)
    state = history
    outputs = []
    for instant in range(STEPS):
        by_block = state.reshape(LAGS, NCB, B, MC)

        def add_group(lag_total, group_index):
            first_row = (group_index * NBLK).astype(jnp.int32)
            rows_of = lax.dynamic_slice_in_dim(global_row, first_row, NBLK)
            lags_of = lax.dynamic_slice_in_dim(global_lag, first_row, NBLK)
            cols_of = lax.dynamic_slice_in_dim(block_col, first_row, NBLK)
            kernels = lax.dynamic_slice_in_dim(kernel_blocks, first_row, NBLK).astype(jnp.float32)
            picked = by_block[lags_of, cols_of].astype(jnp.float32)
            products = jnp.einsum("eij,ejm->eim", kernels, picked, precision=lax.Precision.HIGHEST)
            products = products * mode_kernel[lags_of][:, None, :]
            return lag_total.at[rows_of].add(products), None

        start_total = jnp.zeros((NCB, B, MC), jnp.float32)
        lag_total, unused = lax.scan(add_group, start_total, jnp.arange(BLOCKS // NBLK, dtype=jnp.int32))
        net_field = incident[instant].astype(jnp.float32).reshape(NCB, B, MC) - lag_total
        density = jnp.einsum("cij,cjm->cim", inverse_blocks, net_field, precision=lax.Precision.HIGHEST).reshape(NP, MC)
        outputs.append(density)
        state = jnp.concatenate([density.astype(jnp.bfloat16)[None], state[:-1]], axis=0)
    return jnp.stack(outputs)
```

```python
import functools

import jax
import jax.numpy as jnp
from jax import lax
from jax.experimental import pallas as pl
from jax.experimental.pallas import tpu as pltpu
from jax.sharding import PartitionSpec as P

STEPS = 4
UNROLL = 8
CHUNKS = 4
LIMIT = 40 << 20


def accumulate(out_refs, kernel_of, picks_of, scales_of, first, count):
    def group(g, carry):
        base = first + g * UNROLL
        sums = [[None] * len(refs) for refs in out_refs]
        for u in range(UNROLL):
            entry = base + u
            block = kernel_of(entry)
            picks = picks_of(entry)
            scales = scales_of(entry)
            for k, refs in enumerate(out_refs):
                product = jnp.dot(block, picks[k], preferred_element_type=jnp.float32)
                for r in range(len(refs)):
                    term = product * scales[k][r]
                    sums[k][r] = term if sums[k][r] is None else sums[k][r] + term
        for k, refs in enumerate(out_refs):
            for r, ref in enumerate(refs):
                ref[...] += sums[k][r]
        return carry

    lax.fori_loop(0, count // UNROLL, group, 0)


def chunk_copies(source, target, sems):
    size = source.shape[0] // CHUNKS
    return [
        pltpu.make_async_copy(
            source.at[pl.ds(c * size, size)], target.at[pl.ds(c * size, size)], sems.at[c]
        )
        for c in range(CHUNKS)
    ]


def field_kernel(steps, halo_lags, row_s, col_s, lag_s, blocks_h, *rest):
    if halo_lags:
        halo_h, history_h, mode_ref, out_ref, blocks_v, state_v, sems, state_sem = rest
    else:
        history_h, mode_ref, out_ref, blocks_v, state_v, sems, state_sem = rest
    lags_held = history_h.shape[0]
    copies = [
        pltpu.make_async_copy(
            history_h, state_v.at[pl.ds(halo_lags, lags_held)], state_sem.at[0]
        )
    ]
    if halo_lags:
        copies.append(
            pltpu.make_async_copy(halo_h, state_v.at[pl.ds(0, halo_lags)], state_sem.at[1])
        )
    for copy in copies:
        copy.start()
    block_copies = chunk_copies(blocks_h, blocks_v, sems)
    for copy in block_copies:
        copy.start()
    out_ref[...] = jnp.zeros_like(out_ref)
    size = blocks_v.shape[1]
    row_blocks = out_ref.shape[1]

    def picks_of(entry):
        first = pl.multiple_of(col_s[entry] * size, size)
        lag = lag_s[entry]
        return [state_v[halo_lags + lag - s, pl.ds(first, size), :] for s in steps]

    def scales_of(entry):
        factor = mode_ref[pl.ds(lag_s[entry], 1), :]
        row = row_s[entry]
        own = [jnp.where(row == r, factor, 0.0) for r in range(row_blocks)]
        return [own for _ in steps]

    out_refs = [[out_ref.at[k, r] for r in range(row_blocks)] for k in range(len(steps))]
    for copy in copies:
        copy.wait()
    per = blocks_v.shape[0] // CHUNKS
    for c, copy in enumerate(block_copies):
        copy.wait()
        accumulate(out_refs, lambda e: blocks_v[e], picks_of, scales_of, c * per, per)


def fields(steps, halo, history, kernel_blocks, block_row, block_col, lag_offset, mode_kernel, row_blocks):
    halo_lags = 0 if halo is None else halo.shape[0]
    entries, size, _ = kernel_blocks.shape
    lags_held, points, modes = history.shape
    anywhere = pl.BlockSpec(memory_space=pl.ANY)
    in_smem = pl.BlockSpec(memory_space=pltpu.SMEM)
    in_vmem = pl.BlockSpec(memory_space=pltpu.VMEM)
    states = [history] if halo is None else [halo, history]
    return pl.pallas_call(
        functools.partial(field_kernel, steps, halo_lags),
        out_shape=jax.ShapeDtypeStruct((len(steps), row_blocks, size, modes), jnp.float32),
        in_specs=[in_smem] * 3 + [anywhere] * (1 + len(states)) + [in_vmem],
        out_specs=in_vmem,
        scratch_shapes=[
            pltpu.VMEM(kernel_blocks.shape, kernel_blocks.dtype),
            pltpu.VMEM((halo_lags + lags_held, points, modes), history.dtype),
            pltpu.SemaphoreType.DMA((CHUNKS,)),
            pltpu.SemaphoreType.DMA((2,)),
        ],
        compiler_params=pltpu.CompilerParams(vmem_limit_bytes=LIMIT),
        name=f"fields_{len(steps)}",
    )(block_row, block_col, lag_offset, kernel_blocks, *states, mode_kernel)


def solve_into(inverse_ref, net, density_ref, copies_ref):
    row_blocks, size = net.shape[0], net.shape[1]
    for r in range(row_blocks):
        solved = jnp.dot(
            inverse_ref[pl.ds(r * size, size), :],
            net[r],
            precision=lax.Precision.HIGHEST,
            preferred_element_type=jnp.float32,
        )
        density_ref[pl.ds(r * size, size), :] = solved
        if copies_ref is not None:
            rounded = solved.astype(copies_ref.dtype)
            for p in range(copies_ref.shape[0]):
                copies_ref[p, pl.ds(r * size, size), :] = rounded


def first_kernel(incident_ref, field_ref, inverse_ref, density_ref, copies_ref):
    row_blocks, size, modes = field_ref.shape
    net = incident_ref[...].astype(jnp.float32).reshape(field_ref.shape) - field_ref[...]
    solve_into(inverse_ref, net, density_ref, copies_ref)


def chain_kernel(step, last, row_s, col_s, lag_s, blocks_h, *rest):
    fresh = rest[:step]
    rest = rest[step:]
    if last:
        mode_ref, incident_ref, field_ref, inverse_ref, density_ref, blocks_v, acc, sems = rest
        copies_ref = None
    else:
        mode_ref, incident_ref, field_ref, inverse_ref, density_ref, copies_ref, blocks_v, acc, sems = rest
    size = blocks_v.shape[1]
    row_blocks = acc.shape[0]
    block_copies = chunk_copies(blocks_h, blocks_v, sems)
    for copy in block_copies:
        copy.start()
    acc[...] = jnp.zeros_like(acc)

    def picks_of(entry):
        first = pl.multiple_of(col_s[entry] * size, size)
        lag = lag_s[entry]
        pick = fresh[0][pl.ds(first, size), :]
        for t in range(1, step):
            pick = jnp.where(lag == step - 1 - t, fresh[t][pl.ds(first, size), :], pick)
        return [pick]

    def scales_of(entry):
        lag = lag_s[entry]
        factor = jnp.where(lag < step, mode_ref[pl.ds(lag, 1), :], 0.0)
        row = row_s[entry]
        return [[jnp.where(row == r, factor, 0.0) for r in range(row_blocks)]]

    per = blocks_v.shape[0] // CHUNKS
    for c, copy in enumerate(block_copies):
        copy.wait()
        accumulate(
            [[acc.at[r] for r in range(row_blocks)]],
            lambda e: blocks_v[e],
            picks_of,
            scales_of,
            c * per,
            per,
        )
    net = incident_ref[...].astype(jnp.float32).reshape(acc.shape) - field_ref[...] - acc[...]
    solve_into(inverse_ref, net, density_ref, copies_ref)


def densities_of(step, steps, peers, fresh, incident, field, inverse, tables):
    row_blocks, size, modes = field.shape
    rows = row_blocks * size
    last = step == steps - 1
    in_vmem = pl.BlockSpec(memory_space=pltpu.VMEM)
    in_smem = pl.BlockSpec(memory_space=pltpu.SMEM)
    density = jax.ShapeDtypeStruct((rows, modes), jnp.float32)
    copies = jax.ShapeDtypeStruct((peers, rows, modes), jnp.bfloat16)
    params = pltpu.CompilerParams(vmem_limit_bytes=LIMIT)
    if step == 0:
        return pl.pallas_call(
            first_kernel,
            out_shape=(density, copies),
            in_specs=[in_vmem] * 3,
            out_specs=(in_vmem, in_vmem),
            compiler_params=params,
            name="first_density",
        )(incident, field, inverse)
    block_row, block_col, lag_offset, kernel_blocks, mode_kernel = tables
    return pl.pallas_call(
        functools.partial(chain_kernel, step, last),
        out_shape=(density,) if last else (density, copies),
        in_specs=[in_smem] * 3 + [pl.BlockSpec(memory_space=pl.ANY)] + [in_vmem] * (step + 4),
        out_specs=(in_vmem,) if last else (in_vmem, in_vmem),
        scratch_shapes=[
            pltpu.VMEM(kernel_blocks.shape, kernel_blocks.dtype),
            pltpu.VMEM(field.shape, jnp.float32),
            pltpu.SemaphoreType.DMA((CHUNKS,)),
        ],
        compiler_params=params,
        name=f"chain_{step}",
    )(block_row, block_col, lag_offset, kernel_blocks, *fresh, mode_kernel, incident, field, inverse)


def lag_of(x_hi, z, core):
    return x_hi * 16 + z * 2 + core


TREE = (
    ([(lag_of(x, z, 1), lag_of(x, z, 0)) for x in range(2) for z in range(8)],),
    tuple(
        [(lag_of(x, q + k, 0), lag_of(x, q, 0)) for x in range(2) for q in (0, 4)]
        for k in (1, 2, 3)
    ),
    (
        [(lag_of(0, 4, 0), 0)],
        [(lag_of(1, 0, 0), 0)],
        [(lag_of(1, 4, 0), 0)],
    ),
)


def summed_on_first(value):
    for level in TREE:
        arrived = [lax.ppermute(value, "lag", pairs) for pairs in level]
        for piece in arrived:
            value = value + piece
    return value


def cut_along(value, dim, peers):
    before, after = (value.shape[:dim], value.shape[dim + 1 :])
    return jnp.moveaxis(value.reshape(*before, peers, -1, *after), dim, 0)


def spread_from_first(value):
    peers = lax.axis_size("lag")
    steps, rows, modes = value.shape
    blocks = cut_along(value, 1, peers)
    mine = lax.all_to_all(blocks, "lag", 0, 0, tiled=True)[0]
    everyone = lax.all_to_all(
        jnp.broadcast_to(mine[None], (peers, *mine.shape)), "lag", 0, 0, tiled=True
    )
    return jnp.moveaxis(everyone, 0, 1).reshape(steps, rows, modes)


def per_device(
    history, incident, kernel_blocks, block_row, block_col, lag_offset, mode_kernel, self_inverse
):
    size = kernel_blocks.shape[1]
    rows_here = self_inverse.shape[0]
    row_blocks = rows_here // size
    peers = lax.axis_size("pts")
    lags = lax.axis_size("lag")
    lags_held, points, modes = history.shape
    behind = STEPS - 1
    halo = lax.ppermute(
        history[lags_held - behind :], "lag", [(i, i + 1) for i in range(lags - 1)]
    )
    tables = (block_row, block_col, lag_offset, kernel_blocks, mode_kernel)
    now = fields((0,), None, history, kernel_blocks, block_row, block_col, lag_offset, mode_kernel, row_blocks)
    now = summed_on_first(now[0])
    density, copies = densities_of(0, STEPS, peers, [], incident[0], now, self_inverse, tables)
    later = fields(
        tuple(range(1, STEPS)), halo, history, kernel_blocks, block_row, block_col, lag_offset, mode_kernel, row_blocks
    )
    later = summed_on_first(later)
    fresh = []
    out = [density]
    for step in range(1, STEPS):
        everyone = lax.all_to_all(copies, "pts", 0, 0, tiled=True)
        fresh.append(everyone.reshape(points, modes))
        density, *copies = densities_of(
            step, STEPS, peers, fresh, incident[step], later[step - 1], self_inverse, tables
        )
        copies = copies[0] if copies else None
        out.append(density)
    return spread_from_first(jnp.stack(out))


def solution(mesh):
    return jax.shard_map(
        per_device,
        mesh=mesh,
        in_specs=(
            P("lag", None, None),
            P(None, "pts", None),
            P(("lag", "pts"), None, None),
            P(("lag", "pts")),
            P(("lag", "pts")),
            P(("lag", "pts")),
            P("lag", None),
            P("pts", None),
        ),
        out_specs=P(None, "pts", None),
        check_vma=False,
    )
```

```python
import functools

import jax
import jax.numpy as jnp
from jax import lax
from jax.experimental import pallas as pl
from jax.experimental.pallas import tpu as pltpu
from jax.sharding import PartitionSpec as P


STEPS = 4
UNROLL = 8
CHUNKS = 4
LIMIT = 24 << 20


def accumulate(acc, kernel_of, picks_of, factor_of, row_of, entries):
    steps, row_blocks, _, modes = acc.shape

    sums = [[None] * row_blocks for _ in range(steps)]
    for entry in entries:
        picks = picks_of(entry)
        pick = picks[0] if steps == 1 else jnp.concatenate(picks, axis=1)
        product = jnp.dot(kernel_of(entry), pick, preferred_element_type=jnp.float32)
        factor = factor_of(entry)
        row = row_of(entry)
        for k in range(steps):
            part = product[:, k * modes : (k + 1) * modes]
            if steps > 1:
                acc[k, row] += part * factor
                continue
            for r in range(row_blocks):
                term = part * jnp.where(row == r, factor, 0.0)
                sums[k][r] = term if sums[k][r] is None else sums[k][r] + term
    if steps == 1:
        for r in range(row_blocks):
            acc[0, r] += sums[0][r]


def field_kernel(steps, halo_shapes, row_h, col_h, lag_h, mode_h, blocks_h, history_h, *rest):
    halos = rest[: len(halo_shapes)]
    rest = list(rest[len(halo_shapes) :])
    with_lists = len(steps) == 2
    out_ref = rest.pop(0)
    if with_lists:
        lists_ref = rest.pop(0)
    row_s, col_s, lag_s, mode_ref, acc, blocks_v, state_v, sems, state_sems, table_sems = rest
    table_copies = [
        pltpu.make_async_copy(source, target, table_sems.at[k])
        for k, (source, target) in enumerate(((row_h, row_s), (col_h, col_s), (lag_h, lag_s)))
    ]
    table_copies.append(pltpu.make_async_copy(mode_h, mode_ref, table_sems.at[3]))
    halo_lags = sum(halo_shapes)
    own_lags = state_v.shape[0] - halo_lags
    state_copies = [
        pltpu.make_async_copy(
            history_h.at[pl.ds(0, own_lags)],
            state_v.at[pl.ds(halo_lags, own_lags)],
            state_sems.at[0],
        )
    ]
    first = 0
    for k, halo in enumerate(halos):
        state_copies.append(
            pltpu.make_async_copy(
                halo, state_v.at[pl.ds(first, halo_shapes[k])], state_sems.at[k + 1]
            )
        )
        first += halo_shapes[k]
    for copy in table_copies + state_copies:
        copy.start()
    entries, size, _ = blocks_v.shape
    per = entries // CHUNKS

    def chunk_copy(c):
        part = pl.ds(c * per, per)
        return pltpu.make_async_copy(blocks_h.at[part], blocks_v.at[part], sems.at[c])

    for c in range(CHUNKS):
        chunk_copy(c).start()
    acc[...] = jnp.zeros_like(acc)

    def picks_of(entry):
        first = pl.multiple_of(col_s[entry] * size, size)
        lag = lag_s[entry]
        return [state_v[halo_lags + lag - s, pl.ds(first, size), :] for s in steps]

    def factor_of(entry):
        return mode_ref[pl.ds(lag_s[entry], 1), :]

    for copy in table_copies:
        copy.wait()
    if with_lists:
        kinds = STEPS - 1

        def place(entry, counts):
            lag = lag_s[entry]
            kind = jnp.minimum(lag, kinds)
            at = counts[kinds]
            for j in range(kinds):
                at = jnp.where(lag == j, counts[j], at)
            lists_ref[kind * entries + at] = entry + row_s[entry] * 1024 + col_s[entry] * 65536
            return tuple(count + jnp.where(kind == j, 1, 0) for j, count in enumerate(counts))

        counts = lax.fori_loop(0, entries, place, (jnp.int32(0),) * (kinds + 1))
        for j in range(kinds + 1):
            lists_ref[(kinds + 1) * entries + j] = counts[j]
    for copy in state_copies:
        copy.wait()

    def chunk(c, carry):
        chunk_copy(c).wait()
        accumulate(
            acc,
            lambda e: blocks_v[e],
            picks_of,
            factor_of,
            lambda e: row_s[e],
            [c * per + u for u in range(per)],
        )
        return carry

    lax.fori_loop(0, CHUNKS, chunk, 0)
    if with_lists:
        core = lax.axis_index("lag") % 2
        for k in range(2):
            out_ref[k ^ core] = acc[k]
    else:
        out_ref[...] = acc[...]


def fields(steps, halos, history, tables, row_blocks):
    block_row, block_col, lag_offset, kernel_blocks, mode_kernel = tables
    halo_shapes = tuple(halo.shape[0] for halo in halos)
    entries, size, _ = kernel_blocks.shape
    lags_held, points, modes = history.shape
    in_hbm = pl.BlockSpec(memory_space=pltpu.HBM)
    in_smem = pl.BlockSpec(memory_space=pltpu.SMEM)
    in_vmem = pl.BlockSpec(memory_space=pltpu.VMEM)
    shape = (len(steps), row_blocks, size, modes)
    out_shape = [jax.ShapeDtypeStruct(shape, jnp.float32)]
    out_specs = [in_vmem]
    if len(steps) == 2:
        out_shape.append(jax.ShapeDtypeStruct((STEPS * entries + STEPS,), jnp.int32))
        out_specs.append(in_smem)
    return pl.pallas_call(
        functools.partial(field_kernel, steps, halo_shapes),
        out_shape=out_shape,
        in_specs=[in_hbm] * 6 + [pl.BlockSpec(memory_space=pl.ANY)] * len(halos),
        out_specs=out_specs,
        scratch_shapes=[
            *[pltpu.SMEM((entries,), jnp.int32)] * 3,
            pltpu.VMEM(mode_kernel.shape, jnp.float32),
            pltpu.VMEM(shape, jnp.float32),
            pltpu.VMEM(kernel_blocks.shape, kernel_blocks.dtype),
            pltpu.VMEM((sum(halo_shapes) + lags_held - min(steps), points, modes), history.dtype),
            pltpu.SemaphoreType.DMA((CHUNKS,)),
            pltpu.SemaphoreType.DMA((1 + len(halos),)),
            pltpu.SemaphoreType.DMA((4,)),
        ],
        compiler_params=pltpu.CompilerParams(vmem_limit_bytes=LIMIT),
    )(
        *[
            in_hbm_only(v)
            for v in (block_row, block_col, lag_offset, mode_kernel, kernel_blocks, history)
        ],
        *halos,
    )


def halves(value):
    high = value.astype(jnp.bfloat16)
    return high, (value - high.astype(jnp.float32)).astype(jnp.bfloat16)


def solve_into(inverse_ref, net, density_ref, copies_ref):
    row_blocks, size = net.shape[0], net.shape[1]
    for r in range(row_blocks):
        inverse_high, inverse_low = halves(inverse_ref[pl.ds(r * size, size), :])
        net_high, net_low = halves(net[r])
        solved = jnp.dot(
            jnp.concatenate([inverse_high, inverse_low, inverse_high], axis=1),
            jnp.concatenate([net_low, net_high, net_high], axis=0),
            preferred_element_type=jnp.float32,
        )
        density_ref[pl.ds(r * size, size), :] = solved
        if copies_ref is not None:
            rounded = solved.astype(copies_ref.dtype)
            for p in range(copies_ref.shape[0]):
                copies_ref[p, pl.ds(r * size, size), :] = rounded


def first_kernel(incident_ref, field_ref, inverse_ref, density_ref, copies_ref):
    net = incident_ref[...].astype(jnp.float32).reshape(field_ref.shape) - field_ref[...]
    solve_into(inverse_ref, net, density_ref, copies_ref)


def chain_kernel(step, last, lists_s, blocks_h, *rest):
    fresh = rest[:step]
    rest = rest[step:]
    if last:
        mode_ref, incident_ref, field_ref, inverse_ref, density_ref, blocks_v, acc, sems = rest
        copies_ref = None
    else:
        mode_ref, incident_ref, field_ref, inverse_ref, density_ref, copies_ref, blocks_v, acc, sems = rest
    entries, size, _ = blocks_h.shape
    row_blocks = acc.shape[0]
    counts = [lists_s[STEPS * entries + j] for j in range(step)]
    groups = [(count + UNROLL - 1) // UNROLL for count in counts]
    firsts = [sum(groups[:j]) for j in range(step)]

    def code_of(j, g, u):
        at = g * UNROLL + u
        return at, lists_s[j * entries + jnp.minimum(at, counts[j] - 1)]

    for j in range(step):

        def begin(g, carry, j=j):
            slot = firsts[j] + g
            for u in range(UNROLL):
                _, code = code_of(j, g, u)
                pltpu.make_async_copy(
                    blocks_h.at[code % 1024], blocks_v.at[slot * UNROLL + u], sems.at[slot]
                ).start()
            return carry

        lax.fori_loop(0, groups[j], begin, 0)
    acc[...] = jnp.zeros_like(acc)
    for j in range(step):
        state = fresh[step - 1 - j]
        factor = mode_ref[pl.ds(j, 1), :]

        def group(g, carry, j=j, state=state, factor=factor):
            slot = firsts[j] + g
            pltpu.make_async_copy(
                blocks_h.at[pl.ds(0, UNROLL)], blocks_v.at[pl.ds(slot * UNROLL, UNROLL)], sems.at[slot]
            ).wait()
            sums = [None] * row_blocks
            for u in range(UNROLL):
                at, code = code_of(j, g, u)
                first = pl.multiple_of(code // 65536 * size, size)
                product = jnp.dot(
                    blocks_v[slot * UNROLL + u],
                    state[pl.ds(first, size), :],
                    preferred_element_type=jnp.float32,
                )
                row = jnp.where(at < counts[j], code // 1024 % 64, row_blocks)
                for r in range(row_blocks):
                    term = product * jnp.where(row == r, factor, 0.0)
                    sums[r] = term if sums[r] is None else sums[r] + term
            for r in range(row_blocks):
                acc[r] += sums[r]
            return carry

        lax.fori_loop(0, groups[j], group, 0)
    net = incident_ref[...].astype(jnp.float32).reshape(acc.shape) - field_ref[...] - acc[...]
    solve_into(inverse_ref, net, density_ref, copies_ref)


def densities_of(step, peers, fresh, incident, field, inverse, mode_kernel, blocks, lists):
    row_blocks, size, modes = field.shape
    rows = row_blocks * size
    last = step == STEPS - 1
    in_vmem = pl.BlockSpec(memory_space=pltpu.VMEM)
    in_smem = pl.BlockSpec(memory_space=pltpu.SMEM)
    density = jax.ShapeDtypeStruct((rows, modes), jnp.float32)
    copies = jax.ShapeDtypeStruct((peers, rows, modes), jnp.bfloat16)
    params = pltpu.CompilerParams(vmem_limit_bytes=LIMIT)
    if step == 0:
        return pl.pallas_call(
            first_kernel,
            out_shape=(density, copies),
            in_specs=[in_vmem] * 3,
            out_specs=(in_vmem, in_vmem),
            compiler_params=params,
            name="first_density",
        )(incident, field, inverse)
    slots = blocks.shape[0] // UNROLL + step
    return pl.pallas_call(
        functools.partial(chain_kernel, step, last),
        out_shape=(density,) if last else (density, copies),
        in_specs=[in_smem, pl.BlockSpec(memory_space=pltpu.HBM)] + [in_vmem] * (step + 4),
        out_specs=(in_vmem,) if last else (in_vmem, in_vmem),
        scratch_shapes=[
            pltpu.VMEM(((slots * UNROLL), *blocks.shape[1:]), blocks.dtype),
            pltpu.VMEM(field.shape, jnp.float32),
            pltpu.SemaphoreType.DMA((slots,)),
        ],
        compiler_params=params,
    )(lists, in_hbm_only(blocks), *fresh, mode_kernel, incident, field, inverse)


def lag_of(x_hi, z, core):
    return x_hi * 16 + z % 8 * 2 + core


def routes(cores, pairs):
    return [(lag_of(*a, c), lag_of(*b, c)) for a, b in pairs for c in range(cores)]


BOTH = (0, 1)
TO_CORE_0 = [(lag_of(x, z, 1), lag_of(x, z, 0)) for x in BOTH for z in range(8)]
SWAP = TO_CORE_0 + [(b, a) for a, b in TO_CORE_0]
FROM_CORE_0 = [(b, a) for a, b in TO_CORE_0]
HUBS = [[((x, q + k), (x, q)) for x in BOTH for q in (0, 4)] for k in (1, -1, 2)]
TOPS = [[((0, 4), (0, 0))], [((1, 0), (0, 0))], [((1, 4), (0, 0))]]
ACROSS = [((1, 0), (0, 0)), ((1, 4), (0, 4))]
ALONG = [((0, 4), (0, 0))]


def turned(pairs):
    return [(b, a) for a, b in pairs]


def plus_arrived(value, *levels, operand=None):
    operand = value if operand is None else operand
    arrived = [lax.ppermute(operand, "lag", pairs) for pairs in levels]
    for piece in arrived:
        value = value + piece
    return value


def in_hbm_only(value):
    return pltpu.with_memory_space_constraint(value, pltpu.HBM)


def after(value, other):
    return lax.optimization_barrier((value, other))[0]


def to_everyone(copies):
    everyone = lax.all_to_all(copies, "pts", 0, 0, tiled=True)
    return everyone.reshape(-1, copies.shape[-1])


UP_HUBS = [routes(1, pairs) for pairs in HUBS]
UP_TOPS = [routes(1, pairs) for pairs in TOPS]
DOWN_HUBS = [routes(1, turned(pairs)) for pairs in HUBS]
DOWN_TOPS = [routes(1, turned(pairs)) for pairs in TOPS]


def per_device(
    history, incident, kernel_blocks, block_row, block_col, lag_offset, mode_kernel, self_inverse
):
    size = kernel_blocks.shape[1]
    row_blocks = self_inverse.shape[0] // size
    peers = lax.axis_size("pts")
    lags = lax.axis_size("lag")
    first = lax.axis_index("lag") == 0
    lags_held = history.shape[0]
    next_lag = [(i, i + 1) for i in range(lags - 1)]
    tables = (block_row, block_col, lag_offset, kernel_blocks, mode_kernel)
    halo_1 = lax.ppermute(history[lags_held - 1 :], "lag", next_lag)
    (now,) = fields((0,), [], history, tables, row_blocks)
    now = plus_arrived(now[0], TO_CORE_0)
    halo_2 = lax.ppermute(
        after(history, now)[lags_held - 3 : lags_held - 1], "lag", next_lag
    )
    (second,) = fields((1,), [after(halo_1, now)], history, tables, row_blocks)
    now = plus_arrived(now, *UP_HUBS)
    second = plus_arrived(second[0], TO_CORE_0)
    now = plus_arrived(now, *UP_TOPS)
    second = plus_arrived(second, *UP_HUBS)
    args = (self_inverse, mode_kernel, kernel_blocks)
    density_0, copies = densities_of(0, peers, [], incident[0], now, *args, None)
    fresh = [to_everyone(copies)]
    second = plus_arrived(second, *UP_TOPS)
    pair, lists = fields((2, 3), [after(halo_2, copies), halo_1], history, tables, row_blocks)
    pair = plus_arrived(pair[0], SWAP, operand=pair[1])
    density_1, copies = densities_of(1, peers, fresh, incident[1], second, *args, lists)
    fresh.append(to_everyone(copies))
    pair = after(pair, copies)
    pair = plus_arrived(pair, *[routes(2, pairs) for pairs in HUBS])
    pair = plus_arrived(pair, routes(2, ACROSS))
    pair = plus_arrived(pair, routes(2, ALONG))
    early = jnp.stack([density_0, density_1])
    early = plus_arrived(jnp.where(first, early, 0.0), *DOWN_TOPS, operand=early)
    density_2, copies = densities_of(2, peers, fresh, incident[2], pair, *args, lists)
    fresh.append(to_everyone(copies))
    fourth = lax.ppermute(after(pair, copies), "lag", [(1, 0)])
    third = plus_arrived(jnp.where(first, density_2, 0.0), *DOWN_TOPS, operand=density_2)
    early = plus_arrived(after(early, copies), *DOWN_HUBS)
    early = plus_arrived(early, FROM_CORE_0)
    (density_3,) = densities_of(3, peers, fresh, incident[3], fourth, *args, lists)
    final = plus_arrived(jnp.where(first, density_3, 0.0), *DOWN_TOPS, operand=density_3)
    late = jnp.stack([third, final])
    late = plus_arrived(late, *DOWN_HUBS)
    late = plus_arrived(late, FROM_CORE_0)
    return jnp.concatenate([early, late])


def solution(mesh):
    return jax.shard_map(
        per_device,
        mesh=mesh,
        in_specs=(
            P("lag", None, None),
            P(None, "pts", None),
            P(("lag", "pts"), None, None),
            P(("lag", "pts")),
            P(("lag", "pts")),
            P(("lag", "pts")),
            P("lag", None),
            P("pts", None),
        ),
        out_specs=P(None, "pts", None),
        check_vma=False,
    )
```

```python
import functools

import jax
import jax.numpy as jnp
from jax import lax
from jax.experimental import pallas as pl
from jax.experimental.pallas import tpu as pltpu
from jax.sharding import PartitionSpec as P


STEPS = 4
UNROLL = 8
CHUNKS = 4
LIMIT = 24 << 20
HALO = ((5, 1), (3, 2))


def accumulate(acc, kernel_of, picks_of, factor_of, row_of, entries):
    steps, row_blocks, _, modes = acc.shape

    sums = [[None] * row_blocks for _ in range(steps)]
    for entry in entries:
        picks = picks_of(entry)
        pick = picks[0] if steps == 1 else jnp.concatenate(picks, axis=1)
        product = jnp.dot(kernel_of(entry), pick, preferred_element_type=jnp.float32)
        factor = factor_of(entry)
        row = row_of(entry)
        for k in range(steps):
            part = product[:, k * modes : (k + 1) * modes]
            if steps > 1:
                acc[k, row] += part * factor
                continue
            for r in range(row_blocks):
                term = part * jnp.where(row == r, factor, 0.0)
                sums[k][r] = term if sums[k][r] is None else sums[k][r] + term
    if steps == 1:
        for r in range(row_blocks):
            acc[0, r] += sums[0][r]


def field_kernel(steps, halo_shapes, row_h, col_h, lag_h, mode_h, blocks_h, history_h, *rest):
    halos = rest[: len(halo_shapes)]
    rest = list(rest[len(halo_shapes) :])
    with_lists = len(steps) == 2
    out_ref = rest.pop(0)
    pieces = []
    if with_lists:
        lists_ref = rest.pop(0)
    if not halos:
        pieces = [rest.pop(0) for _ in HALO]
    row_s, col_s, lag_s, mode_ref, acc, blocks_v, state_v, sems, state_sems, table_sems, *piece_sems = rest
    table_copies = [
        pltpu.make_async_copy(source, target, table_sems.at[k])
        for k, (source, target) in enumerate(((row_h, row_s), (col_h, col_s), (lag_h, lag_s)))
    ]
    table_copies.append(pltpu.make_async_copy(mode_h, mode_ref, table_sems.at[3]))
    halo_lags = sum(halo_shapes)
    own_lags = state_v.shape[0] - halo_lags
    state_copies = [
        pltpu.make_async_copy(
            history_h.at[pl.ds(0, own_lags)],
            state_v.at[pl.ds(halo_lags, own_lags)],
            state_sems.at[0],
        )
    ]
    first = 0
    for k, halo in enumerate(halos):
        state_copies.append(
            pltpu.make_async_copy(
                halo, state_v.at[pl.ds(first, halo_shapes[k])], state_sems.at[k + 1]
            )
        )
        first += halo_shapes[k]
    for copy in table_copies + state_copies:
        copy.start()
    entries, size, _ = blocks_v.shape
    per = entries // CHUNKS

    def chunk_copy(c):
        part = pl.ds(c * per, per)
        return pltpu.make_async_copy(blocks_h.at[part], blocks_v.at[part], sems.at[c])

    for c in range(CHUNKS):
        chunk_copy(c).start()
    acc[...] = jnp.zeros_like(acc)

    def picks_of(entry):
        first = pl.multiple_of(col_s[entry] * size, size)
        lag = lag_s[entry]
        return [state_v[halo_lags + lag - s, pl.ds(first, size), :] for s in steps]

    def factor_of(entry):
        return mode_ref[pl.ds(lag_s[entry], 1), :]

    for copy in table_copies:
        copy.wait()
    kinds = STEPS - 1

    def place(entry, counts):
        lag = lag_s[entry]
        kind = jnp.minimum(lag, kinds)
        at = counts[kinds]
        for j in range(kinds):
            at = jnp.where(lag == j, counts[j], at)
        lists_ref[kind * entries + at] = entry + row_s[entry] * 1024 + col_s[entry] * 65536
        return tuple(count + jnp.where(kind == j, 1, 0) for j, count in enumerate(counts))

    for copy in state_copies:
        copy.wait()

    piece_copies = [
        pltpu.make_async_copy(
            state_v.at[pl.ds(start, count)], piece, piece_sems[0].at[k]
        )
        for k, (piece, (start, count)) in enumerate(zip(pieces, HALO))
    ]
    for copy in piece_copies:
        copy.start()

    def chunk(c, counts):
        chunk_copy(c).wait()
        run = [c * per + u for u in range(per)]
        if with_lists:
            for entry in run:
                counts = place(entry, counts)
        accumulate(acc, lambda e: blocks_v[e], picks_of, factor_of, lambda e: row_s[e], run)
        return counts

    counts = lax.fori_loop(0, CHUNKS, chunk, (jnp.int32(0),) * (kinds + 1) if with_lists else ())
    for j, count in enumerate(counts):
        lists_ref[(kinds + 1) * entries + j] = count
    for copy in piece_copies:
        copy.wait()
    if with_lists:
        core = lax.axis_index("lag") % 2
        for k in range(2):
            out_ref[k ^ core] = acc[k]
    else:
        out_ref[...] = acc[...]


def fields(steps, halos, history, tables, row_blocks):
    block_row, block_col, lag_offset, kernel_blocks, mode_kernel = tables
    halo_shapes = tuple(halo.shape[0] for halo in halos)
    entries, size, _ = kernel_blocks.shape
    lags_held, points, modes = history.shape
    in_hbm = pl.BlockSpec(memory_space=pltpu.HBM)
    in_smem = pl.BlockSpec(memory_space=pltpu.SMEM)
    in_vmem = pl.BlockSpec(memory_space=pltpu.VMEM)
    shape = (len(steps), row_blocks, size, modes)
    out_shape = [jax.ShapeDtypeStruct(shape, jnp.float32)]
    out_specs = [in_vmem]
    if len(steps) == 2:
        out_shape.append(jax.ShapeDtypeStruct((STEPS * entries + STEPS,), jnp.int32))
        out_specs.append(in_smem)
    more_scratch = []
    if not halos:
        out_shape += [
            jax.ShapeDtypeStruct((count, points, modes), history.dtype) for _, count in HALO
        ]
        out_specs += [in_hbm] * len(HALO)
        more_scratch.append(pltpu.SemaphoreType.DMA((len(HALO),)))
    return pl.pallas_call(
        functools.partial(field_kernel, steps, halo_shapes),
        out_shape=out_shape,
        in_specs=[in_hbm] * 6 + [pl.BlockSpec(memory_space=pl.ANY)] * len(halos),
        out_specs=out_specs,
        scratch_shapes=[
            *[pltpu.SMEM((entries,), jnp.int32)] * 3,
            pltpu.VMEM(mode_kernel.shape, jnp.float32),
            pltpu.VMEM(shape, jnp.float32),
            pltpu.VMEM(kernel_blocks.shape, kernel_blocks.dtype),
            pltpu.VMEM((sum(halo_shapes) + lags_held - min(steps), points, modes), history.dtype),
            pltpu.SemaphoreType.DMA((CHUNKS,)),
            pltpu.SemaphoreType.DMA((1 + len(halos),)),
            pltpu.SemaphoreType.DMA((4,)),
            *more_scratch,
        ],
        compiler_params=pltpu.CompilerParams(vmem_limit_bytes=LIMIT),
    )(
        *[
            in_hbm_only(v)
            for v in (block_row, block_col, lag_offset, mode_kernel, kernel_blocks, history)
        ],
        *halos,
    )


def halves(value):
    high = value.astype(jnp.bfloat16)
    return high, (value - high.astype(jnp.float32)).astype(jnp.bfloat16)


def solve_into(inverse_ref, net, density_ref, copies_ref):
    row_blocks, size = net.shape[0], net.shape[1]
    for r in range(row_blocks):
        inverse_high, inverse_low = halves(inverse_ref[pl.ds(r * size, size), :])
        net_high, net_low = halves(net[r])
        solved = jnp.dot(
            jnp.concatenate([inverse_high, inverse_low, inverse_high], axis=1),
            jnp.concatenate([net_low, net_high, net_high], axis=0),
            preferred_element_type=jnp.float32,
        )
        density_ref[pl.ds(r * size, size), :] = solved
        if copies_ref is not None:
            rounded = solved.astype(copies_ref.dtype)
            for p in range(copies_ref.shape[0]):
                copies_ref[p, pl.ds(r * size, size), :] = rounded


def first_kernel(incident_ref, field_ref, inverse_ref, density_ref, copies_ref):
    net = incident_ref[...].astype(jnp.float32).reshape(field_ref.shape) - field_ref[...]
    solve_into(inverse_ref, net, density_ref, copies_ref)


def chain_kernel(step, last, lists_s, blocks_h, *rest):
    fresh = rest[:step]
    rest = rest[step:]
    if last:
        mode_ref, incident_ref, field_ref, inverse_ref, density_ref, blocks_v, acc, sems = rest
        copies_ref = None
    else:
        mode_ref, incident_ref, field_ref, inverse_ref, density_ref, copies_ref, blocks_v, acc, sems = rest
    entries, size, _ = blocks_h.shape
    row_blocks = acc.shape[0]
    counts = [lists_s[STEPS * entries + j] for j in range(step)]
    root = lax.axis_index("lag") == 0
    groups = [jnp.where(root, (count + UNROLL - 1) // UNROLL, 0) for count in counts]
    firsts = [sum(groups[:j]) for j in range(step)]

    def code_of(j, g, u):
        at = g * UNROLL + u
        return at, lists_s[j * entries + jnp.minimum(at, counts[j] - 1)]

    for j in range(step):

        def begin(g, carry, j=j):
            slot = firsts[j] + g
            for u in range(UNROLL):
                _, code = code_of(j, g, u)
                pltpu.make_async_copy(
                    blocks_h.at[code % 1024], blocks_v.at[slot * UNROLL + u], sems.at[slot]
                ).start()
            return carry

        lax.fori_loop(0, groups[j], begin, 0)
    acc[...] = jnp.zeros_like(acc)
    for j in range(step):
        state = fresh[step - 1 - j]
        factor = mode_ref[pl.ds(j, 1), :]

        def group(g, carry, j=j, state=state, factor=factor):
            slot = firsts[j] + g
            pltpu.make_async_copy(
                blocks_h.at[pl.ds(0, UNROLL)], blocks_v.at[pl.ds(slot * UNROLL, UNROLL)], sems.at[slot]
            ).wait()
            sums = [None] * row_blocks
            for u in range(UNROLL):
                at, code = code_of(j, g, u)
                first = pl.multiple_of(code // 65536 * size, size)
                product = jnp.dot(
                    blocks_v[slot * UNROLL + u],
                    state[pl.ds(first, size), :],
                    preferred_element_type=jnp.float32,
                )
                row = jnp.where(at < counts[j], code // 1024 % 64, row_blocks)
                for r in range(row_blocks):
                    term = product * jnp.where(row == r, factor, 0.0)
                    sums[r] = term if sums[r] is None else sums[r] + term
            for r in range(row_blocks):
                acc[r] += sums[r]
            return carry

        lax.fori_loop(0, groups[j], group, 0)
    net = incident_ref[...].astype(jnp.float32).reshape(acc.shape) - field_ref[...] - acc[...]
    solve_into(inverse_ref, net, density_ref, copies_ref)


def densities_of(step, peers, fresh, incident, field, inverse, mode_kernel, blocks, lists):
    row_blocks, size, modes = field.shape
    rows = row_blocks * size
    last = step == STEPS - 1
    in_vmem = pl.BlockSpec(memory_space=pltpu.VMEM)
    in_smem = pl.BlockSpec(memory_space=pltpu.SMEM)
    density = jax.ShapeDtypeStruct((rows, modes), jnp.float32)
    copies = jax.ShapeDtypeStruct((peers, rows, modes), jnp.bfloat16)
    params = pltpu.CompilerParams(vmem_limit_bytes=LIMIT)
    if step == 0:
        return pl.pallas_call(
            first_kernel,
            out_shape=(density, copies),
            in_specs=[in_vmem] * 3,
            out_specs=(in_vmem, in_vmem),
            compiler_params=params,
            name="first_density",
        )(incident, field, inverse)
    slots = blocks.shape[0] // UNROLL + step
    return pl.pallas_call(
        functools.partial(chain_kernel, step, last),
        out_shape=(density,) if last else (density, copies),
        in_specs=[in_smem, pl.BlockSpec(memory_space=pltpu.HBM)] + [in_vmem] * (step + 4),
        out_specs=(in_vmem,) if last else (in_vmem, in_vmem),
        scratch_shapes=[
            pltpu.VMEM(((slots * UNROLL), *blocks.shape[1:]), blocks.dtype),
            pltpu.VMEM(field.shape, jnp.float32),
            pltpu.SemaphoreType.DMA((slots,)),
        ],
        compiler_params=params,
    )(lists, in_hbm_only(blocks), *fresh, mode_kernel, incident, field, inverse)


def lag_of(x_hi, z, core):
    return x_hi * 16 + z % 8 * 2 + core


def routes(cores, pairs):
    return [(lag_of(*a, c), lag_of(*b, c)) for a, b in pairs for c in cores]


BOTH = (0, 1)
TO_CORE_0 = [(lag_of(x, z, 1), lag_of(x, z, 0)) for x in BOTH for z in range(8)]
TO_CORE_1 = [(b, a) for a, b in TO_CORE_0]
SWAP = TO_CORE_0 + TO_CORE_1
HUBS = [[((x, q + k), (x, q)) for x in BOTH for q in (0, 4)] for k in (1, -1, 2)]
TOPS = [[((0, 4), (0, 0))], [((1, 0), (0, 0))], [((1, 4), (0, 0))]]
HALVES = [
    [((x, z + 1), (x, z)) for x in BOTH for z in (0, 2, 4, 6)],
    [((x, z + 2), (x, z)) for x in BOTH for z in (0, 4)],
    [((x, 4), (x, 0)) for x in BOTH],
    [((1, 0), (0, 0))],
]
ASIDE = [
    [((1, z + 1), (1, z)) for z in (0, 2, 4, 6)] + [((0, z), (0, z + 1)) for z in (2, 4, 6)],
    [((1, z + 2), (1, z)) for z in (0, 4)] + [((0, z + 3), (0, z + 1)) for z in (0, 4)],
    [((1, 4), (1, 0)), ((0, 5), (0, 1))],
    [((1, 0), (0, 1))],
]


def turned(pairs):
    return [(b, a) for a, b in pairs]


def plus_arrived(value, *levels, operand=None):
    operand = value if operand is None else operand
    arrived = [lax.ppermute(operand, "lag", pairs) for pairs in levels]
    for piece in arrived:
        value = value + piece
    return value


def in_hbm_only(value):
    return pltpu.with_memory_space_constraint(value, pltpu.HBM)


def after(value, other):
    return lax.optimization_barrier((value, other))[0]


def to_everyone(copies):
    everyone = lax.all_to_all(copies, "pts", 0, 0, tiled=True)
    return everyone.reshape(-1, copies.shape[-1])


def on_core(core, value, other):
    return jnp.where(lax.axis_index("lag") % 2 == core, value, other)


def per_device(
    history, incident, kernel_blocks, block_row, block_col, lag_offset, mode_kernel, self_inverse
):
    size = kernel_blocks.shape[1]
    row_blocks = self_inverse.shape[0] // size
    peers = lax.axis_size("pts")
    lags = lax.axis_size("lag")
    first = lax.axis_index("lag") == 0
    next_lag = [(i, i + 1) for i in range(lags - 1)]
    tables = (block_row, block_col, lag_offset, kernel_blocks, mode_kernel)
    now, piece_1, piece_2 = fields((0,), [], history, tables, row_blocks)
    now = plus_arrived(now[0], TO_CORE_0)
    halo_1 = lax.ppermute(piece_1, "lag", next_lag)
    halo_2 = lax.ppermute(piece_2, "lag", next_lag)
    now = plus_arrived(now, *[routes((0,), pairs) for pairs in HUBS])
    (second,) = fields((1,), [after(halo_1, now)], history, tables, row_blocks)
    now = plus_arrived(now, *[routes((0,), pairs) for pairs in TOPS])
    second = plus_arrived(second[0], TO_CORE_1)
    args = (self_inverse, mode_kernel, kernel_blocks)
    density_0, copies = densities_of(0, peers, [], incident[0], now, *args, None)
    fresh = [to_everyone(copies)]
    for pairs in HALVES:
        second = plus_arrived(second, routes((1,), pairs))
    second = lax.ppermute(second, "lag", [(1, 0)])
    pair, lists = fields((2, 3), [after(halo_2, copies), halo_1], history, tables, row_blocks)
    pair = plus_arrived(pair[0], SWAP, operand=pair[1])
    for pairs in ASIDE:
        pair = plus_arrived(pair, routes(BOTH, pairs))
    density_1, copies = densities_of(1, peers, fresh, incident[1], second, *args, lists)
    fresh.append(to_everyone(copies))
    pair = plus_arrived(pair, routes(BOTH, [((0, 1), (0, 0))]), operand=after(pair, copies))
    early = jnp.stack([density_0, density_1])
    moving = lax.ppermute(early, "lag", [(0, 1)])
    for pairs in HALVES[::-1]:
        moving = plus_arrived(moving, routes((1,), turned(pairs)))
    density_2, copies = densities_of(2, peers, fresh, incident[2], pair, *args, lists)
    fresh.append(to_everyone(copies))
    fourth = lax.ppermute(after(pair, copies), "lag", [(1, 0)])
    third = lax.ppermute(density_2, "lag", [(0, 1)])
    for pairs in HALVES[:1:-1]:
        third = plus_arrived(third, routes((1,), turned(pairs)))
    arrived = lax.ppermute(moving, "lag", TO_CORE_0[1:])
    early = jnp.where(first, early, on_core(0, arrived, moving))
    (density_3,) = densities_of(3, peers, fresh, incident[3], fourth, *args, lists)
    final = plus_arrived(
        jnp.where(first, density_3, 0.0),
        *[routes((0,), turned(pairs)) for pairs in TOPS],
        operand=density_3,
    )
    late = plus_arrived(on_core(0, final, third), *[routes(BOTH, turned(pairs)) for pairs in HUBS])
    other = lax.ppermute(late, "lag", SWAP)
    late = jnp.stack([on_core(0, other, late), on_core(0, late, other)])
    return jnp.concatenate([early, late])


def solution(mesh):
    return jax.shard_map(
        per_device,
        mesh=mesh,
        in_specs=(
            P("lag", None, None),
            P(None, "pts", None),
            P(("lag", "pts"), None, None),
            P(("lag", "pts")),
            P(("lag", "pts")),
            P(("lag", "pts")),
            P("lag", None),
            P("pts", None),
        ),
        out_specs=P(None, "pts", None),
        check_vma=False,
    )
```

```python
import functools

import jax
import jax.numpy as jnp
from jax import lax
from jax.experimental import pallas as pl
from jax.experimental.pallas import tpu as pltpu
from jax.sharding import PartitionSpec as P


STEPS = 4
UNROLL = 8
CHUNKS = 4
LIMIT = 24 << 20
HALO = ((5, 1), (3, 2))


def accumulate(acc, kernel_of, picks_of, factor_of, row_of, entries):
    steps, row_blocks, _, modes = acc.shape

    sums = [[None] * row_blocks for _ in range(steps)]
    for entry in entries:
        picks = picks_of(entry)
        pick = picks[0] if steps == 1 else jnp.concatenate(picks, axis=1)
        product = jnp.dot(kernel_of(entry), pick, preferred_element_type=jnp.float32)
        factor = factor_of(entry)
        row = row_of(entry)
        for k in range(steps):
            part = product[:, k * modes : (k + 1) * modes]
            if steps > 1:
                acc[k, row] += part * factor
                continue
            for r in range(row_blocks):
                term = part * jnp.where(row == r, factor, 0.0)
                sums[k][r] = term if sums[k][r] is None else sums[k][r] + term
    if steps == 1:
        for r in range(row_blocks):
            acc[0, r] += sums[0][r]


def field_kernel(steps, halo_shapes, row_h, col_h, lag_h, mode_h, blocks_h, history_h, *rest):
    halos = rest[: len(halo_shapes)]
    rest = list(rest[len(halo_shapes) :])
    with_lists = len(steps) == 2
    out_ref = rest.pop(0)
    pieces = []
    if with_lists:
        lists_ref = rest.pop(0)
    if not halos:
        pieces = [rest.pop(0) for _ in HALO]
    row_s, col_s, lag_s, mode_ref, acc, blocks_v, state_v, sems, state_sems, table_sems, *piece_sems = rest
    table_copies = [
        pltpu.make_async_copy(source, target, table_sems.at[k])
        for k, (source, target) in enumerate(((row_h, row_s), (col_h, col_s), (lag_h, lag_s)))
    ]
    table_copies.append(pltpu.make_async_copy(mode_h, mode_ref, table_sems.at[3]))
    halo_lags = sum(halo_shapes)
    own_lags = state_v.shape[0] - halo_lags
    state_copies = [
        pltpu.make_async_copy(
            history_h.at[pl.ds(0, own_lags)],
            state_v.at[pl.ds(halo_lags, own_lags)],
            state_sems.at[0],
        )
    ]
    first = 0
    for k, halo in enumerate(halos):
        state_copies.append(
            pltpu.make_async_copy(
                halo, state_v.at[pl.ds(first, halo_shapes[k])], state_sems.at[k + 1]
            )
        )
        first += halo_shapes[k]
    for copy in table_copies + state_copies:
        copy.start()
    entries, size, _ = blocks_v.shape
    per = entries // CHUNKS

    def chunk_copy(c):
        part = pl.ds(c * per, per)
        return pltpu.make_async_copy(blocks_h.at[part], blocks_v.at[part], sems.at[c])

    for c in range(CHUNKS):
        chunk_copy(c).start()
    acc[...] = jnp.zeros_like(acc)

    def picks_of(entry):
        first = pl.multiple_of(col_s[entry] * size, size)
        lag = lag_s[entry]
        return [state_v[halo_lags + lag - s, pl.ds(first, size), :] for s in steps]

    def factor_of(entry):
        return mode_ref[pl.ds(lag_s[entry], 1), :]

    for copy in table_copies:
        copy.wait()
    kinds = STEPS - 1

    def place(entry, counts):
        lag = lag_s[entry]
        kind = jnp.minimum(lag, kinds)
        at = counts[kinds]
        for j in range(kinds):
            at = jnp.where(lag == j, counts[j], at)
        lists_ref[kind * entries + at] = entry + row_s[entry] * 1024 + col_s[entry] * 65536
        return tuple(count + jnp.where(kind == j, 1, 0) for j, count in enumerate(counts))

    for copy in state_copies:
        copy.wait()

    piece_copies = [
        pltpu.make_async_copy(
            state_v.at[pl.ds(start, count)], piece, piece_sems[0].at[k]
        )
        for k, (piece, (start, count)) in enumerate(zip(pieces, HALO))
    ]
    for copy in piece_copies:
        copy.start()

    def chunk(c, counts):
        chunk_copy(c).wait()
        run = [c * per + u for u in range(per)]
        if with_lists:
            for entry in run:
                counts = place(entry, counts)
        accumulate(acc, lambda e: blocks_v[e], picks_of, factor_of, lambda e: row_s[e], run)
        return counts

    counts = lax.fori_loop(0, CHUNKS, chunk, (jnp.int32(0),) * (kinds + 1) if with_lists else ())
    for j, count in enumerate(counts):
        lists_ref[(kinds + 1) * entries + j] = count
    for copy in piece_copies:
        copy.wait()
    if with_lists:
        core = lax.axis_index("lag") % 2
        for k in range(2):
            out_ref[k ^ core] = acc[k]
    else:
        out_ref[...] = acc[...]


def fields(steps, halos, history, tables, row_blocks):
    block_row, block_col, lag_offset, kernel_blocks, mode_kernel = tables
    halo_shapes = tuple(halo.shape[0] for halo in halos)
    entries, size, _ = kernel_blocks.shape
    lags_held, points, modes = history.shape
    in_hbm = pl.BlockSpec(memory_space=pltpu.HBM)
    in_smem = pl.BlockSpec(memory_space=pltpu.SMEM)
    in_vmem = pl.BlockSpec(memory_space=pltpu.VMEM)
    shape = (len(steps), row_blocks, size, modes)
    out_shape = [jax.ShapeDtypeStruct(shape, jnp.float32)]
    out_specs = [in_vmem]
    if len(steps) == 2:
        out_shape.append(jax.ShapeDtypeStruct((STEPS * entries + STEPS,), jnp.int32))
        out_specs.append(in_smem)
    more_scratch = []
    if not halos:
        out_shape += [
            jax.ShapeDtypeStruct((count, points, modes), history.dtype) for _, count in HALO
        ]
        out_specs += [in_hbm] * len(HALO)
        more_scratch.append(pltpu.SemaphoreType.DMA((len(HALO),)))
    return pl.pallas_call(
        functools.partial(field_kernel, steps, halo_shapes),
        out_shape=out_shape,
        in_specs=[in_hbm] * 6 + [pl.BlockSpec(memory_space=pl.ANY)] * len(halos),
        out_specs=out_specs,
        scratch_shapes=[
            *[pltpu.SMEM((entries,), jnp.int32)] * 3,
            pltpu.VMEM(mode_kernel.shape, jnp.float32),
            pltpu.VMEM(shape, jnp.float32),
            pltpu.VMEM(kernel_blocks.shape, kernel_blocks.dtype),
            pltpu.VMEM((sum(halo_shapes) + lags_held - min(steps), points, modes), history.dtype),
            pltpu.SemaphoreType.DMA((CHUNKS,)),
            pltpu.SemaphoreType.DMA((1 + len(halos),)),
            pltpu.SemaphoreType.DMA((4,)),
            *more_scratch,
        ],
        compiler_params=pltpu.CompilerParams(vmem_limit_bytes=LIMIT),
    )(
        *[
            in_hbm_only(v)
            for v in (block_row, block_col, lag_offset, mode_kernel, kernel_blocks, history)
        ],
        *halos,
    )


def halves(value):
    high = value.astype(jnp.bfloat16)
    return high, (value - high.astype(jnp.float32)).astype(jnp.bfloat16)


def solve_into(inverse_ref, net, density_ref, copies_ref):
    row_blocks, size = net.shape[0], net.shape[1]
    for r in range(row_blocks):
        inverse_high, inverse_low = halves(inverse_ref[pl.ds(r * size, size), :])
        net_high, net_low = halves(net[r])
        solved = jnp.dot(
            jnp.concatenate([inverse_high, inverse_low, inverse_high], axis=1),
            jnp.concatenate([net_low, net_high, net_high], axis=0),
            preferred_element_type=jnp.float32,
        )
        density_ref[pl.ds(r * size, size), :] = solved
        if copies_ref is not None:
            rounded = solved.astype(copies_ref.dtype)
            for p in range(copies_ref.shape[0]):
                copies_ref[p, pl.ds(r * size, size), :] = rounded


def first_kernel(incident_ref, field_ref, inverse_ref, density_ref, copies_ref):
    net = incident_ref[...].astype(jnp.float32).reshape(field_ref.shape) - field_ref[...]
    solve_into(inverse_ref, net, density_ref, copies_ref)


def chain_kernel(lags, ahead, last, lists_s, blocks_h, *rest):
    step = len(lags)
    fresh = rest[:step]
    rest = rest[step:]
    copies_ref = None
    if ahead:
        mode_ref, sum_ref, blocks_v, acc, sems = rest
    elif last:
        mode_ref, incident_ref, field_ref, inverse_ref, density_ref, blocks_v, acc, sems = rest
    else:
        mode_ref, incident_ref, field_ref, inverse_ref, density_ref, copies_ref, blocks_v, acc, sems = rest
    entries, size, _ = blocks_h.shape
    row_blocks = acc.shape[0]
    counts = [lists_s[STEPS * entries + j] for j in lags]
    root = lax.axis_index("lag") == 0
    groups = [jnp.where(root, (count + UNROLL - 1) // UNROLL, 0) for count in counts]
    firsts = [sum(groups[:j]) for j in range(step)]

    def code_of(j, g, u):
        at = g * UNROLL + u
        return at, lists_s[lags[j] * entries + jnp.minimum(at, counts[j] - 1)]

    for j in range(step):

        def begin(g, carry, j=j):
            slot = firsts[j] + g
            for u in range(UNROLL):
                _, code = code_of(j, g, u)
                pltpu.make_async_copy(
                    blocks_h.at[code % 1024], blocks_v.at[slot * UNROLL + u], sems.at[slot]
                ).start()
            return carry

        lax.fori_loop(0, groups[j], begin, 0)
    acc[...] = jnp.zeros_like(acc)
    for j in range(step):
        state = fresh[j]
        factor = mode_ref[pl.ds(lags[j], 1), :]

        def group(g, carry, j=j, state=state, factor=factor):
            slot = firsts[j] + g
            pltpu.make_async_copy(
                blocks_h.at[pl.ds(0, UNROLL)], blocks_v.at[pl.ds(slot * UNROLL, UNROLL)], sems.at[slot]
            ).wait()
            sums = [None] * row_blocks
            for u in range(UNROLL):
                at, code = code_of(j, g, u)
                first = pl.multiple_of(code // 65536 * size, size)
                product = jnp.dot(
                    blocks_v[slot * UNROLL + u],
                    state[pl.ds(first, size), :],
                    preferred_element_type=jnp.float32,
                )
                row = jnp.where(at < counts[j], code // 1024 % 64, row_blocks)
                for r in range(row_blocks):
                    term = product * jnp.where(row == r, factor, 0.0)
                    sums[r] = term if sums[r] is None else sums[r] + term
            for r in range(row_blocks):
                acc[r] += sums[r]
            return carry

        lax.fori_loop(0, groups[j], group, 0)
    if ahead:
        sum_ref[...] = acc[...]
        return
    net = incident_ref[...].astype(jnp.float32).reshape(acc.shape) - field_ref[...] - acc[...]
    solve_into(inverse_ref, net, density_ref, copies_ref)


def densities_of(step, peers, fresh, incident, field, inverse, mode_kernel, blocks, lists):
    row_blocks, size, modes = field.shape
    rows = row_blocks * size
    last = step == STEPS - 1
    in_vmem = pl.BlockSpec(memory_space=pltpu.VMEM)
    in_smem = pl.BlockSpec(memory_space=pltpu.SMEM)
    density = jax.ShapeDtypeStruct((rows, modes), jnp.float32)
    copies = jax.ShapeDtypeStruct((peers, rows, modes), jnp.bfloat16)
    params = pltpu.CompilerParams(vmem_limit_bytes=LIMIT)
    if step == 0:
        return pl.pallas_call(
            first_kernel,
            out_shape=(density, copies),
            in_specs=[in_vmem] * 3,
            out_specs=(in_vmem, in_vmem),
            compiler_params=params,
            name="first_density",
        )(incident, field, inverse)
    sum_shape = (rows // size, size, modes)

    def call(lags, ahead, states, more):
        slots = blocks.shape[0] // UNROLL + len(lags)
        if ahead:
            out_shape = (jax.ShapeDtypeStruct(sum_shape, jnp.float32),)
        else:
            out_shape = (density,) if last else (density, copies)
        return pl.pallas_call(
            functools.partial(chain_kernel, lags, ahead, last),
            out_shape=out_shape,
            in_specs=[in_smem, pl.BlockSpec(memory_space=pltpu.HBM)]
            + [in_vmem] * (len(states) + 1 + len(more)),
            out_specs=(in_vmem,) * len(out_shape),
            scratch_shapes=[
                pltpu.VMEM(((slots * UNROLL), *blocks.shape[1:]), blocks.dtype),
                pltpu.VMEM(sum_shape, jnp.float32),
                pltpu.SemaphoreType.DMA((slots,)),
            ],
            compiler_params=params,
        )(lists, in_hbm_only(blocks), *states, mode_kernel, *more)

    if step > 1:
        (old,) = call(tuple(range(1, step)), True, fresh[step - 2 :: -1], ())
        field = field + old
    return call((0,), False, fresh[-1:], (incident, field, inverse))


def lag_of(x_hi, z, core):
    return x_hi * 16 + z % 8 * 2 + core


def routes(cores, pairs):
    return [(lag_of(*a, c), lag_of(*b, c)) for a, b in pairs for c in cores]


BOTH = (0, 1)
TO_CORE_0 = [(lag_of(x, z, 1), lag_of(x, z, 0)) for x in BOTH for z in range(8)]
TO_CORE_1 = [(b, a) for a, b in TO_CORE_0]
SWAP = TO_CORE_0 + TO_CORE_1
HUBS = [[((x, q + k), (x, q)) for x in BOTH for q in (0, 4)] for k in (1, -1, 2)]
TOPS = [[((0, 4), (0, 0))], [((1, 0), (0, 0))], [((1, 4), (0, 0))]]
HALVES = [
    [((x, z + 1), (x, z)) for x in BOTH for z in (0, 2, 4, 6)],
    [((x, z + 2), (x, z)) for x in BOTH for z in (0, 4)],
    [((x, 4), (x, 0)) for x in BOTH],
    [((1, 0), (0, 0))],
]
ASIDE = [
    [((1, z + 1), (1, z)) for z in (0, 2, 4, 6)] + [((0, z), (0, z + 1)) for z in (2, 4, 6)],
    [((1, z + 2), (1, z)) for z in (0, 4)] + [((0, z + 3), (0, z + 1)) for z in (0, 4)],
    [((1, 4), (1, 0)), ((0, 5), (0, 1))],
    [((1, 0), (0, 1))],
]


def turned(pairs):
    return [(b, a) for a, b in pairs]


def plus_arrived(value, *levels, operand=None):
    operand = value if operand is None else operand
    arrived = [lax.ppermute(operand, "lag", pairs) for pairs in levels]
    for piece in arrived:
        value = value + piece
    return value


def in_hbm_only(value):
    return pltpu.with_memory_space_constraint(value, pltpu.HBM)


def after(value, other):
    return lax.optimization_barrier((value, other))[0]


def to_everyone(copies):
    everyone = lax.all_to_all(copies, "pts", 0, 0, tiled=True)
    return everyone.reshape(-1, copies.shape[-1])


def on_core(core, value, other):
    return jnp.where(lax.axis_index("lag") % 2 == core, value, other)


def per_device(
    history, incident, kernel_blocks, block_row, block_col, lag_offset, mode_kernel, self_inverse
):
    size = kernel_blocks.shape[1]
    row_blocks = self_inverse.shape[0] // size
    peers = lax.axis_size("pts")
    lags = lax.axis_size("lag")
    first = lax.axis_index("lag") == 0
    next_lag = [(i, i + 1) for i in range(lags - 1)]
    tables = (block_row, block_col, lag_offset, kernel_blocks, mode_kernel)
    now, piece_1, piece_2 = fields((0,), [], history, tables, row_blocks)
    now = plus_arrived(now[0], TO_CORE_0)
    halo_1 = lax.ppermute(piece_1, "lag", next_lag)
    halo_2 = lax.ppermute(piece_2, "lag", next_lag)
    now = plus_arrived(now, *[routes((0,), pairs) for pairs in HUBS])
    (second,) = fields((1,), [after(halo_1, now)], history, tables, row_blocks)
    now = plus_arrived(now, *[routes((0,), pairs) for pairs in TOPS])
    second = plus_arrived(second[0], TO_CORE_1)
    args = (self_inverse, mode_kernel, kernel_blocks)
    density_0, copies = densities_of(0, peers, [], incident[0], now, *args, None)
    fresh = [to_everyone(copies)]
    for pairs in HALVES:
        second = plus_arrived(second, routes((1,), pairs))
    second = lax.ppermute(second, "lag", [(1, 0)])
    pair, lists = fields((2, 3), [after(halo_2, copies), halo_1], history, tables, row_blocks)
    pair = plus_arrived(pair[0], SWAP, operand=pair[1])
    for pairs in ASIDE:
        pair = plus_arrived(pair, routes(BOTH, pairs))
    density_1, copies = densities_of(1, peers, fresh, incident[1], second, *args, lists)
    fresh.append(to_everyone(copies))
    pair = plus_arrived(pair, routes(BOTH, [((0, 1), (0, 0))]), operand=after(pair, copies))
    early = jnp.stack([density_0, density_1])
    moving = lax.ppermute(early, "lag", [(0, 1)])
    for pairs in HALVES[::-1]:
        moving = plus_arrived(moving, routes((1,), turned(pairs)))
    density_2, copies = densities_of(2, peers, fresh, incident[2], pair, *args, lists)
    fresh.append(to_everyone(copies))
    fourth = lax.ppermute(after(pair, copies), "lag", [(1, 0)])
    third = lax.ppermute(density_2, "lag", [(0, 1)])
    for pairs in HALVES[:1:-1]:
        third = plus_arrived(third, routes((1,), turned(pairs)))
    arrived = lax.ppermute(moving, "lag", TO_CORE_0[1:])
    early = jnp.where(first, early, on_core(0, arrived, moving))
    (density_3,) = densities_of(3, peers, fresh, incident[3], fourth, *args, lists)
    final = plus_arrived(
        jnp.where(first, density_3, 0.0),
        *[routes((0,), turned(pairs)) for pairs in TOPS],
        operand=density_3,
    )
    late = plus_arrived(on_core(0, final, third), *[routes(BOTH, turned(pairs)) for pairs in HUBS])
    other = lax.ppermute(late, "lag", SWAP)
    late = jnp.stack([on_core(0, other, late), on_core(0, late, other)])
    return jnp.concatenate([early, late])


def solution(mesh):
    return jax.shard_map(
        per_device,
        mesh=mesh,
        in_specs=(
            P("lag", None, None),
            P(None, "pts", None),
            P(("lag", "pts"), None, None),
            P(("lag", "pts")),
            P(("lag", "pts")),
            P(("lag", "pts")),
            P("lag", None),
            P("pts", None),
        ),
        out_specs=P(None, "pts", None),
        check_vma=False,
    )
```
